512 devices in a mesh: grp: 8 (over y, core), row: 64 (over z, x).
Axes of the slice: x: 4, y: 4, z: 16, core: 2. Of those that a mesh axis runs over, the one named last changes fastest.
Arguments:
- test_panel: bfloat16 [64, 1048576], P(None, ('grp', 'row')), may hold values from -6 to 6
- node_scale: float32 [1048576], P(('grp', 'row')), may hold values from 0.3 to 5.2
- diag_blocks: bfloat16 [64, 1048576], P(None, ('grp', 'row')), may hold values from -0.3125 to 0.3125
- off_blocks: bfloat16 [5, 64, 1048576], P(None, None, ('grp', 'row')), may hold values from -0.3125 to 0.3125
- block_columns: int32 [5, 16384], P(None, ('grp', 'row')), may hold values from 0 to 127, as said below
- send_lists: int32 [32768, 2], P(('grp', 'row')), may hold values from -1 to 31, as said below
Outputs:
- basis_panel: float32 [64, 1048576], P(None, ('grp', 'row'))
- r_factor: float32 [64, 64], replicated
The draws below stay inside these ranges and needn't reach their ends.
Inputs may be any that keep to these rules, and one draw needn't show every extreme that they name: `send_lists`: row r of a device's list holds, in its first entries, distinct local block rows of that device whose panel blocks device r of the same group along row reads, and -1 in the rest. A row for a device at cycle distance at most 3 along row (wrapping within the group, the device itself included) holds 1 to 2 blocks; the row for the device itself always holds exactly 2, and one more near row may hold 2; a row for a farther device holds exactly one block. `block_columns`: entry (k, b) = s * 2 + j names entry j of the list that device s of the reader's group along row holds for the reader; that entry is never -1. Every live entry of the lists held for a device is named by some entry of that device's block rows.
All inputs are finite; a program needn't handle non-finite values.
Results may differ from the reference program's by a relative error of at most 0.003.
Values may be sent and summed in bfloat16 or wider, within the bound.
No kernel may reach another device: no remote copies, remote signals or barrier semaphores. Data moves between devices by JAX's collectives and lax.ppermute only.
A program may use at most 64 MiB of HBM per device.

```python
import math
import jax
import jax.numpy as jnp
from jax import lax

BLOCK = 64
PANEL = 64
OFFDIAG = 5
CAPACITY = 2
BLOCK_ROWS = 32
NODES = 1048576
N_GRP = 8
N_ROW = 64


def block_pattern(key):
    devices_all = N_GRP * N_ROW
    dest_rank = jnp.arange(devices_all, dtype=jnp.int32) % N_ROW
    source_rank = jnp.arange(N_ROW, dtype=jnp.int32)
    cycle_step = (source_rank[None, :] - dest_rank[:, None]) % N_ROW
    cycle_dist = jnp.minimum(cycle_step, N_ROW - cycle_step)
    is_near = cycle_dist <= 3
    near_count = jax.random.randint(jax.random.fold_in(key, 11), (devices_all, N_ROW), 1, CAPACITY + 1)
    counts = jnp.where(is_near, near_count, 1)
    full_shift = jax.random.randint(jax.random.fold_in(key, 13), (devices_all,), -3, 4)
    full_peer = (dest_rank + full_shift) % N_ROW
    is_full = (source_rank[None, :] == full_peer[:, None]) | (cycle_dist == 0)
    counts = jnp.where(is_full, CAPACITY, counts).astype(jnp.int32)
    list_keys = jax.random.split(jax.random.fold_in(key, 14), devices_all * N_ROW)
    orders = jax.vmap(lambda one_key: jax.random.permutation(one_key, BLOCK_ROWS))(list_keys)
    orders = orders[:, :CAPACITY].astype(jnp.int32).reshape(devices_all, N_ROW, CAPACITY)
    slot_index = jnp.arange(CAPACITY, dtype=jnp.int32)
    is_live = slot_index[None, None, :] < counts[:, :, None]
    lists_for = jnp.where(is_live, orders, -1).astype(jnp.int32)
    slot_value = source_rank[None, :, None] * CAPACITY + slot_index[None, None, :]
    slot_value = jnp.broadcast_to(slot_value, (devices_all, N_ROW, CAPACITY)).astype(jnp.int32)
    block_offsets = jnp.cumsum(counts, axis=1) - counts
    position = jnp.where(is_live, block_offsets[:, :, None] + slot_index[None, None, :], N_ROW * CAPACITY)
    device_rows = jnp.broadcast_to(jnp.arange(devices_all, dtype=jnp.int32)[:, None, None], position.shape)
    compact = jnp.zeros((devices_all, N_ROW * CAPACITY + 1), jnp.int32)
    compact = compact.at[device_rows, position].set(slot_value, mode='drop')
    totals = jnp.sum(counts, axis=1)
    refs_all = BLOCK_ROWS * OFFDIAG
    ref_keys = jax.random.split(jax.random.fold_in(key, 15), devices_all)
    shuffle = jax.vmap(lambda one_key: jax.random.permutation(one_key, refs_all))(ref_keys).astype(jnp.int32)
    picked = shuffle % totals[:, None]
    assigned = jnp.take_along_axis(compact, picked, axis=1)
    columns_out = assigned.reshape(devices_all, BLOCK_ROWS, OFFDIAG).transpose(2, 0, 1).reshape(OFFDIAG, devices_all * BLOCK_ROWS)
    lists_out = lists_for.reshape(N_GRP, N_ROW, N_ROW, CAPACITY).transpose(0, 2, 1, 3).reshape(devices_all * N_ROW, CAPACITY)
    return (lists_out.astype(jnp.int32), columns_out.astype(jnp.int32))


def draw_send_lists(key, part):
    return block_pattern(key)[0]


def draw_block_columns(key, part):
    return block_pattern(key)[1]


def draw_node_scale(key, part):
    along = jnp.arange(NODES, dtype=jnp.float32) / NODES
    trend = jnp.sqrt(1.0 + 2.0 * along)
    rough = jnp.exp(jax.random.uniform(key, (NODES,), jnp.float32, math.log(0.3), math.log(3.0)))
    return (trend * rough).astype(jnp.float32)


def block_scale(stream_key, shape, shards, low, high):
    gain, own = 1.0, jax.random.fold_in(stream_key, 6)
    for dim, parts in shards:
        draws = jnp.exp(jax.random.uniform(jax.random.fold_in(own, dim), (parts,), jnp.float32, low / len(shards), high / len(shards)))
        gain = gain * jnp.repeat(draws, shape[dim] // parts).reshape([-1 if axis == dim else 1 for axis in range(len(shape))])
    return gain


def noise(key, shape, spread, limit, pieces=(), kind=jnp.bfloat16):
    drawn = spread * jax.random.normal(key, shape, jnp.float32)
    if pieces:
        drawn = drawn * block_scale(key, shape, pieces, -0.22, 0.18)
    return jnp.clip(drawn, -limit, limit).astype(kind)


def setup_inputs(seed: int = 0) -> dict:
    streams_of = jax.random.split(jax.random.key(seed), 7)
    return {
        "test_panel": noise(streams_of[0], (PANEL, NODES), 1.0, 6.0, ((1, 512),)),
        "node_scale": draw_node_scale(jax.random.fold_in(streams_of[6], 71), 0),
        "diag_blocks": noise(streams_of[2], (BLOCK, NODES), ((OFFDIAG + 1) * BLOCK) ** -0.5, 0.3125, ((1, 512),)),
        "off_blocks": noise(streams_of[3], (OFFDIAG, BLOCK, NODES), ((OFFDIAG + 1) * BLOCK) ** -0.5, 0.3125, ((2, 512),)),
        "block_columns": draw_block_columns(jax.random.fold_in(streams_of[6], 71), 0),
        "send_lists": draw_send_lists(jax.random.fold_in(streams_of[6], 71), 0),
    }


def reference(test_panel, node_scale, diag_blocks, off_blocks, block_columns, send_lists):
    node_total = test_panel.shape[1]
    block_total = node_total // BLOCK
    scaled = (test_panel.astype(jnp.float32) * node_scale[None, :]).astype(jnp.bfloat16)
    by_block = scaled.astype(jnp.float32).reshape(PANEL, block_total, BLOCK)
    row_device = jnp.arange(block_total, dtype=jnp.int32) // BLOCK_ROWS
    group_base = row_device // N_ROW * N_ROW
    reader = row_device % N_ROW
    source = group_base[None, :] + block_columns // CAPACITY
    list_row = source * N_ROW + reader[None, :]
    selected_blocks = send_lists[list_row, block_columns % CAPACITY]
    column_block = (source * BLOCK_ROWS + selected_blocks).astype(jnp.int32)
    diag_view = diag_blocks.reshape(BLOCK, block_total, BLOCK)
    off_view = off_blocks.reshape(OFFDIAG, BLOCK, block_total, BLOCK)

    def one_device(start_block):
        resident_panel = lax.dynamic_slice_in_dim(by_block, start_block, BLOCK_ROWS, 1)
        local_diagonal = lax.dynamic_slice_in_dim(diag_view, start_block, BLOCK_ROWS, 1).astype(jnp.float32)
        iteration_output = jnp.einsum('mik,kif->mif', resident_panel, local_diagonal, precision=lax.Precision.HIGHEST)
        cols_here = lax.dynamic_slice_in_dim(column_block, start_block, BLOCK_ROWS, 1)
        remote = jnp.take(by_block, cols_here, axis=1)
        off_here = lax.dynamic_slice_in_dim(off_view, start_block, BLOCK_ROWS, 2).astype(jnp.float32)
        return iteration_output + jnp.einsum('pkbc,kcbn->pbn', remote, off_here, precision=lax.Precision.HIGHEST)
    block_offsets = jnp.arange(block_total // BLOCK_ROWS, dtype=jnp.int32) * BLOCK_ROWS
    per_device = lax.map(one_device, block_offsets)
    product = per_device.transpose(1, 0, 2, 3).reshape(PANEL, node_total)
    sketch = product * node_scale[None, :]
    reduced_gram_matrix = jnp.dot(sketch, sketch.T, precision=lax.Precision.HIGHEST) / node_total
    factor_low = jnp.linalg.cholesky(reduced_gram_matrix)
    basis_panel = lax.linalg.triangular_solve(factor_low, sketch, left_side=True, lower=True)
    return (basis_panel, factor_low.T)
```

```python
import jax
import jax.numpy as jnp
from jax import lax
from jax.experimental import pallas as pl
from jax.experimental.pallas import tpu as pltpu
from jax.sharding import Mesh, PartitionSpec as P

NY, NC, NZ, NX = 4, 2, 16, 4
PLANE = ("y", "c", "x")
NPLANE = NY * NC * NX
MIB = 1 << 20


def vmem():
    return pl.BlockSpec(memory_space=pltpu.VMEM)


def smem():
    return pl.BlockSpec(memory_space=pltpu.SMEM)


def left_half(rows):
    return lax.broadcasted_iota(jnp.int32, (rows, 128), 1) < 64


def pack_kernel(lists, panel, scale, scaled, payload, blocks):
    left = left_half(32)
    for i in range(panel.shape[1] // 128):
        cols = slice(128 * i, 128 * i + 128)
        slab = panel[:, cols].astype(jnp.float32) * scale[i : i + 1, :]
        scaled[:, cols] = slab.astype(jnp.bfloat16)
        top, low = slab[:32], slab[32:]
        even = jnp.where(left, top, pltpu.roll(low, 64, 1))
        odd = jnp.where(left, pltpu.roll(top, 64, 1), low)
        blocks[2 * i] = even.astype(jnp.bfloat16)
        blocks[2 * i + 1] = odd.astype(jnp.bfloat16)
    z, x = lax.axis_index("z"), lax.axis_index("x")
    rank = z * NX + x
    for to in range(NX):
        for zz in range(NZ):
            payload[to, zz] = blocks[jnp.maximum(lists[zz * NX + to, 0], 0)]
        step = lax.rem(to - x + NX, NX)
        first = lax.rem(rank + step, NZ * NX)
        second = lax.rem(rank + step - NX + NZ * NX, NZ * NX)
        payload[to, NZ] = blocks[jnp.maximum(lists[first, 1], 0)]
        payload[to, NZ + 1] = blocks[jnp.maximum(lists[second, 1], 0)]


def multiply_kernel(where_at, main, near, above, below, scaled, scale, diag, off, halves, gram, table):
    left = left_half(32)

    def spread(at, packed):
        wide = packed.astype(jnp.float32)
        turned = pltpu.roll(wide, 64, 1)
        table[at, :32] = jnp.where(left, wide, turned).astype(jnp.bfloat16)
        table[at, 32:] = jnp.where(left, turned, wide).astype(jnp.bfloat16)

    for s in range(NZ * NX):
        spread(s, main[s // NX, s % NX])
    for s in range(NX):
        spread(64 + s, near[s, 0])
        spread(68 + s, near[s, 1])
        spread(72 + s, above[s])
        spread(76 + s, below[s])

    left64 = left_half(64)
    same = (lax.broadcasted_iota(jnp.int32, (128, 128), 0) < 64) == left_half(128)
    zero = jnp.zeros((), jnp.bfloat16)
    total = jnp.zeros((128, 128), jnp.float32)
    for i in range(scaled.shape[1] // 128):
        cols = slice(128 * i, 128 * i + 128)
        own = diag[:, cols]
        own = jnp.where(same, jnp.concatenate([own, own], axis=0), zero)
        product = jnp.dot(scaled[:, cols], own, preferred_element_type=jnp.float32)
        rows = []
        for b in (2 * i, 2 * i + 1):
            read = [table[where_at[k, b]] for k in range(5)]
            first = jnp.where(left64, read[0], read[1])
            second = jnp.where(left64, read[2], read[3])
            third = jnp.where(left64, read[4], zero)
            rows.append(jnp.concatenate([first, second, third], axis=1))
        weights = [off[k, :, cols] for k in range(5)]
        weights.append(jnp.zeros((64, 128), jnp.bfloat16))
        both = jnp.dot(
            jnp.concatenate(rows, axis=0),
            jnp.concatenate(weights, axis=0),
            preferred_element_type=jnp.float32,
        )
        product = product + jnp.where(left64, both[:64], both[64:])
        sketch = product * scale[i : i + 1, :]
        high = sketch.astype(jnp.bfloat16)
        low = (sketch - high.astype(jnp.float32)).astype(jnp.bfloat16)
        pair = jnp.concatenate([high, low], axis=0)
        halves[:, cols] = pair
        total = total + lax.dot_general(
            pair, pair, (((1,), (1,)), ((), ())), preferred_element_type=jnp.float32
        )
    total = total[:64] + total[64:]
    total = total + pltpu.roll(total, 64, 1)
    gram[:, 0, :] = jnp.where(left, total[:32], total[32:])


def finish_kernel(node_count, gram, halves, basis, factor):
    packed = gram[:, 0, :] * (1.0 / node_count)
    turned = pltpu.roll(packed, 64, 1)
    full = jnp.concatenate([packed, turned], axis=0)
    lane = lax.broadcasted_iota(jnp.int32, (64, 128), 1)
    row = lax.broadcasted_iota(jnp.int32, (64, 128), 0)
    work = jnp.where(lane < 64, full, (lane - 64 == row).astype(jnp.float32))
    for k in range(64):
        column = jnp.broadcast_to(work[:, k : k + 1], (64, 128))
        pivot = column[k : k + 1, :]
        inverse = lax.rsqrt(pivot)
        inverse = inverse * (1.5 - 0.5 * pivot * inverse * inverse)
        scaled_row = work[k : k + 1, :] * inverse
        factor_column = column * inverse
        work = jnp.where(
            row > k, work - factor_column * scaled_row, jnp.where(row == k, scaled_row, work)
        )
    factor[...] = jnp.where(row <= lane, work, 0.0)[:, :64]
    solve = pltpu.roll(work, 64, 1)
    solve = jnp.where((lane < 64) & (lane <= row), solve, 0.0)
    high = solve.astype(jnp.bfloat16)
    low = (solve - high.astype(jnp.float32)).astype(jnp.bfloat16)
    twice = jnp.where(lane < 64, solve, pltpu.roll(solve, 64, 1)).astype(jnp.bfloat16)
    left = jnp.concatenate([twice, low], axis=0)
    for i in range(halves.shape[1] // 256):
        cols = slice(256 * i, 256 * i + 256)
        both = jnp.dot(left, halves[:, cols], preferred_element_type=jnp.float32)
        basis[:, cols] = both[:64] + both[64:]


def shards(test_panel, node_scale, diag_blocks, off_blocks, block_columns, send_lists):
    panel_width, local_nodes = test_panel.shape
    node_count = local_nodes * NY * NC * NZ * NX
    scale = node_scale.reshape(local_nodes // 128, 128)
    scaled, payload = pl.pallas_call(
        pack_kernel,
        out_shape=(
            jax.ShapeDtypeStruct((64, local_nodes), jnp.bfloat16),
            jax.ShapeDtypeStruct((NX, NZ + 2, 32, 128), jnp.bfloat16),
        ),
        in_specs=[smem(), vmem(), vmem()],
        out_specs=(vmem(), vmem()),
        scratch_shapes=[pltpu.VMEM((32, 32, 128), jnp.bfloat16)],
        compiler_params=pltpu.CompilerParams(vmem_limit_bytes=8 * MIB),
        name="pack",
    )(send_lists, test_panel, scale)

    z, x = lax.axis_index("z"), lax.axis_index("x")
    source, entry = block_columns // 2, block_columns % 2
    source_z, source_x = source // NX, source % NX
    same = 64 + jnp.where(source_x <= x, source_x, NX + source_x)
    other = jnp.where(source_z == (z + NZ - 1) % NZ, 72, 76) + source_x
    where_at = jnp.where(entry == 0, source, jnp.where(source_z == z, same, other))

    near = lax.all_to_all(payload, "x", 0, 0, tiled=True)
    up = [(i, (i + 1) % NZ) for i in range(NZ)]
    down = [((i + 1) % NZ, i) for i in range(NZ)]
    above = lax.ppermute(near[:, NZ], "z", up)
    below = lax.ppermute(near[:, NZ + 1], "z", down)
    main = lax.all_to_all(near[:, :NZ].transpose(1, 0, 2, 3), "z", 0, 0, tiled=True)

    halves, gram = pl.pallas_call(
        multiply_kernel,
        out_shape=(
            jax.ShapeDtypeStruct((128, local_nodes), jnp.bfloat16),
            jax.ShapeDtypeStruct((32, 1, 128), jnp.float32),
        ),
        in_specs=[smem()] + [vmem()] * 8,
        out_specs=(vmem(), vmem()),
        scratch_shapes=[pltpu.VMEM((80, 64, 128), jnp.bfloat16)],
        compiler_params=pltpu.CompilerParams(vmem_limit_bytes=16 * MIB),
        name="multiply",
    )(where_at, main, near[:, NZ:], above, below, scaled, scale, diag_blocks, off_blocks)

    part = lax.all_to_all(gram, PLANE, 0, 0, tiled=True).sum(0)
    part = lax.all_to_all(jnp.broadcast_to(part[None], (NZ, 1, 128)), "z", 0, 0, tiled=True).sum(0)
    gram = lax.all_to_all(jnp.broadcast_to(part[None], (NPLANE, 1, 128)), PLANE, 0, 0, tiled=True)

    def finish(*refs):
        finish_kernel(node_count, *refs)

    return pl.pallas_call(
        finish,
        out_shape=(
            jax.ShapeDtypeStruct((64, local_nodes), jnp.float32),
            jax.ShapeDtypeStruct((64, 64), jnp.float32),
        ),
        in_specs=[vmem(), vmem()],
        out_specs=(vmem(), vmem()),
        compiler_params=pltpu.CompilerParams(vmem_limit_bytes=8 * MIB),
        name="finish",
    )(gram, halves)


def solution(mesh):
    split = Mesh(mesh.devices.reshape(NY, NC, NZ, NX), ("y", "c", "z", "x"))
    every = ("y", "c", "z", "x")
    in_specs = (
        P(None, every),
        P(every),
        P(None, every),
        P(None, None, every),
        P(None, every),
        P(every, None),
    )
    out_specs = (P(None, every), P())
    return jax.shard_map(shards, mesh=split, in_specs=in_specs, out_specs=out_specs, check_vma=False)
```

```python
import jax
import jax.numpy as jnp
from jax import lax
from jax.experimental import pallas as pl
from jax.experimental.pallas import tpu as pltpu
from jax.sharding import Mesh, PartitionSpec as P

NY, NC, NZ, NX = 4, 2, 16, 4
PLANE = ("y", "c", "x")
NPLANE = NY * NC * NX
MIB = 1 << 20


def vmem():
    return pl.BlockSpec(memory_space=pltpu.VMEM)


def smem():
    return pl.BlockSpec(memory_space=pltpu.SMEM)


def outside():
    return pl.BlockSpec(memory_space=pltpu.HBM)


def anywhere():
    return pl.BlockSpec(memory_space=pl.ANY)


def left_half(rows):
    return lax.broadcasted_iota(jnp.int32, (rows, 128), 1) < 64


def pack_kernel(lists_at, panel_at, scale_at, scaled, payload, extra, lists, panel, scale, blocks, sems):
    fetches = [
        pltpu.make_async_copy(scale_at, scale, sems.at[0]),
        pltpu.make_async_copy(panel_at, panel, sems.at[1]),
        pltpu.make_async_copy(lists_at, lists, sems.at[2]),
    ]
    for fetch in fetches:
        fetch.start()
    for fetch in fetches:
        fetch.wait()
    left = left_half(32)
    for i in range(panel.shape[1] // 128):
        cols = slice(128 * i, 128 * i + 128)
        slab = panel[:, cols].astype(jnp.float32) * scale[i : i + 1, :]
        scaled[:, cols] = slab.astype(jnp.bfloat16)
        top, low = slab[:32], slab[32:]
        even = jnp.where(left, top, pltpu.roll(low, 64, 1))
        odd = jnp.where(left, pltpu.roll(top, 64, 1), low)
        blocks[2 * i] = even.astype(jnp.bfloat16)
        blocks[2 * i + 1] = odd.astype(jnp.bfloat16)
    z, x = lax.axis_index("z"), lax.axis_index("x")
    rank = z * NX + x
    for to in range(NX):
        for zz in range(NZ):
            payload[zz * NX + to] = blocks[jnp.maximum(lists[0, zz * NX + to], 0)]
        step = lax.rem(to - x + NX, NX)
        first = lax.rem(rank + step, NZ * NX)
        second = lax.rem(rank + step - NX + NZ * NX, NZ * NX)
        extra[jnp.bitwise_xor(to, x), 0] = blocks[jnp.maximum(lists[1, first], 0)]
        extra[jnp.bitwise_xor(to, x), 1] = blocks[jnp.maximum(lists[1, second], 0)]


def multiply_kernel(where_at, main, near, above, below, scaled, scale, diag, off, halves, gram, table):
    left = left_half(32)

    def spread(at, packed):
        wide = packed.astype(jnp.float32)
        turned = pltpu.roll(wide, 64, 1)
        table[at, :32] = jnp.where(left, wide, turned).astype(jnp.bfloat16)
        table[at, 32:] = jnp.where(left, turned, wide).astype(jnp.bfloat16)

    for s in range(NZ * NX):
        spread(s, main[s])
    for s in range(NX):
        spread(64 + s, near[s, 0])
        spread(68 + s, near[s, 1])
        spread(72 + s, above[s])
        spread(76 + s, below[s])

    left64 = left_half(64)
    same = (lax.broadcasted_iota(jnp.int32, (128, 128), 0) < 64) == left_half(128)
    zero = jnp.zeros((), jnp.bfloat16)
    total = jnp.zeros((128, 128), jnp.float32)
    for i in range(scaled.shape[1] // 128):
        cols = slice(128 * i, 128 * i + 128)
        own = diag[:, cols]
        own = jnp.where(same, jnp.concatenate([own, own], axis=0), zero)
        product = jnp.dot(scaled[:, cols], own, preferred_element_type=jnp.float32)
        rows = []
        for b in (2 * i, 2 * i + 1):
            read = [table[where_at[k, b]] for k in range(5)]
            first = jnp.where(left64, read[0], read[1])
            second = jnp.where(left64, read[2], read[3])
            third = jnp.where(left64, read[4], zero)
            rows.append(jnp.concatenate([first, second, third], axis=1))
        weights = [off[k, :, cols] for k in range(5)]
        weights.append(jnp.zeros((64, 128), jnp.bfloat16))
        both = jnp.dot(
            jnp.concatenate(rows, axis=0),
            jnp.concatenate(weights, axis=0),
            preferred_element_type=jnp.float32,
        )
        product = product + jnp.where(left64, both[:64], both[64:])
        sketch = product * scale[i : i + 1, :]
        high = sketch.astype(jnp.bfloat16)
        low = (sketch - high.astype(jnp.float32)).astype(jnp.bfloat16)
        pair = jnp.concatenate([high, low], axis=0)
        halves[:, cols] = pair
        total = total + lax.dot_general(
            pair, pair, (((1,), (1,)), ((), ())), preferred_element_type=jnp.float32
        )
    total = total[:64] + total[64:]
    total = total + pltpu.roll(total, 64, 1)
    gram[:, 0, :] = jnp.where(left, total[:32], total[32:])


def factor_rows(blocks):
    sub = lax.broadcasted_iota(jnp.int32, (8, 128), 0)
    for p in range(8):
        columns = [
            [jnp.broadcast_to(blocks[r][:, 8 * p + j : 8 * p + j + 1], (8, 128)) for r in range(p, 8)]
            for j in range(8)
        ]
        for j in range(8):
            pivot = jnp.broadcast_to(columns[j][0][j : j + 1], (8, 128))
            inverse = lax.rsqrt(pivot)
            inverse = inverse * (1.5 - 0.5 * pivot * inverse * inverse)
            ratio = [c * inverse for c in columns[j]]
            ratio[0] = jnp.where(sub > j, ratio[0], 0.0)
            for t in range(j + 1, 8):
                lead = jnp.broadcast_to(columns[t][0][j : j + 1], (8, 128)) * inverse
                columns[t] = [c - f * lead for c, f in zip(columns[t], ratio)]
            lead = jnp.broadcast_to(blocks[p][j : j + 1], (8, 128)) * inverse
            for r in range(p, 8):
                blocks[r] = blocks[r] - ratio[r - p] * lead
            blocks[p] = jnp.where(sub == j, lead, blocks[p])
    return jnp.concatenate(blocks, axis=0)


def finish_kernel(node_count, gram, halves, basis_at, factor, basis, sems):
    packed = gram[:, 0, :] * (1.0 / node_count)
    turned = pltpu.roll(packed, 64, 1)
    full = jnp.concatenate([packed, turned], axis=0)
    lane = lax.broadcasted_iota(jnp.int32, (64, 128), 1)
    row = lax.broadcasted_iota(jnp.int32, (64, 128), 0)
    work = jnp.where(lane < 64, full, (lane - 64 == row).astype(jnp.float32))
    work = factor_rows([work[8 * r : 8 * r + 8] for r in range(8)])
    factor[...] = jnp.where(row <= lane, work, 0.0)[:, :64]
    solve = pltpu.roll(work, 64, 1)
    solve = jnp.where((lane < 64) & (lane <= row), solve, 0.0)
    high = solve.astype(jnp.bfloat16)
    low = (solve - high.astype(jnp.float32)).astype(jnp.bfloat16)
    twice = jnp.where(lane < 64, solve, pltpu.roll(solve, 64, 1)).astype(jnp.bfloat16)
    left = jnp.concatenate([twice, low], axis=0)
    stores = []
    for i in range(halves.shape[1] // 256):
        cols = slice(256 * i, 256 * i + 256)
        both = jnp.dot(left, halves[:, cols], preferred_element_type=jnp.float32)
        basis[:, cols] = both[:64] + both[64:]
        stores.append(pltpu.make_async_copy(basis.at[:, cols], basis_at.at[:, cols], sems.at[i]))
        stores[-1].start()
    for store in stores:
        store.wait()


def shards(test_panel, node_scale, diag_blocks, off_blocks, block_columns, send_lists):
    panel_width, local_nodes = test_panel.shape
    node_count = local_nodes * NY * NC * NZ * NX
    scale = node_scale.reshape(local_nodes // 128, 128)
    scaled, payload, extra = pl.pallas_call(
        pack_kernel,
        out_shape=(
            jax.ShapeDtypeStruct((64, local_nodes), jnp.bfloat16),
            jax.ShapeDtypeStruct((NZ * NX, 32, 128), jnp.bfloat16),
            jax.ShapeDtypeStruct((NX, 2, 32, 128), jnp.bfloat16),
        ),
        in_specs=[outside(), outside(), outside()],
        out_specs=(vmem(), vmem(), vmem()),
        scratch_shapes=[
            pltpu.SMEM((2, NZ * NX), jnp.int32),
            pltpu.VMEM((64, local_nodes), jnp.bfloat16),
            pltpu.VMEM((local_nodes // 128, 128), jnp.float32),
            pltpu.VMEM((32, 32, 128), jnp.bfloat16),
            pltpu.SemaphoreType.DMA((3,)),
        ],
        name="pack",
    )(send_lists.T, test_panel, scale)

    z, x = lax.axis_index("z"), lax.axis_index("x")
    source, entry = block_columns // 2, block_columns % 2
    source_z, source_x = source // NX, source % NX
    apart = source_x ^ x
    same = 64 + jnp.where(source_x <= x, apart, NX + apart)
    other = jnp.where(source_z == (z + NZ - 1) % NZ, 72, 76) + apart
    where_at = jnp.where(entry == 0, source, jnp.where(source_z == z, same, other))

    main = lax.all_to_all(payload, ("z", "x"), 0, 0, tiled=True)
    moved = [lax.ppermute(extra[d], "x", [(i, i ^ d) for i in range(NX)]) for d in (1, 2, 3)]
    near = jnp.stack([extra[0]] + moved)
    up = [(i, (i + 1) % NZ) for i in range(NZ)]
    down = [((i + 1) % NZ, i) for i in range(NZ)]
    above = lax.ppermute(near[:, 0], "z", up)
    below = lax.ppermute(near[:, 1], "z", down)

    halves, gram = pl.pallas_call(
        multiply_kernel,
        out_shape=(
            jax.ShapeDtypeStruct((128, local_nodes), jnp.bfloat16),
            jax.ShapeDtypeStruct((32, 1, 128), jnp.float32),
        ),
        in_specs=[smem()] + [vmem()] * 8,
        out_specs=(vmem(), vmem()),
        scratch_shapes=[pltpu.VMEM((80, 64, 128), jnp.bfloat16)],
        compiler_params=pltpu.CompilerParams(vmem_limit_bytes=16 * MIB),
        name="multiply",
    )(where_at, main, near, above, below, scaled, scale, diag_blocks, off_blocks)

    part = lax.all_to_all(gram, PLANE, 0, 0, tiled=True).sum(0)
    part = lax.all_to_all(jnp.broadcast_to(part[None], (NZ, 1, 128)), "z", 0, 0, tiled=True).sum(0)
    gram = lax.all_to_all(jnp.broadcast_to(part[None], (NPLANE, 1, 128)), PLANE, 0, 0, tiled=True)

    def finish(*refs):
        finish_kernel(node_count, *refs)

    return pl.pallas_call(
        finish,
        out_shape=(
            jax.ShapeDtypeStruct((64, local_nodes), jnp.float32),
            jax.ShapeDtypeStruct((64, 64), jnp.float32),
        ),
        in_specs=[vmem(), vmem()],
        out_specs=(anywhere(), vmem()),
        scratch_shapes=[
            pltpu.VMEM((64, local_nodes), jnp.float32),
            pltpu.SemaphoreType.DMA((local_nodes // 256,)),
        ],
        compiler_params=pltpu.CompilerParams(vmem_limit_bytes=8 * MIB),
        name="finish",
    )(gram, halves)


def solution(mesh):
    split = Mesh(mesh.devices.reshape(NY, NC, NZ, NX), ("y", "c", "z", "x"))
    every = ("y", "c", "z", "x")
    in_specs = (
        P(None, every),
        P(every),
        P(None, every),
        P(None, None, every),
        P(None, every),
        P(every, None),
    )
    out_specs = (P(None, every), P())
    return jax.shard_map(shards, mesh=split, in_specs=in_specs, out_specs=out_specs, check_vma=False)
```

```python
import jax
import jax.numpy as jnp
from jax import lax
from jax.experimental import pallas as pl
from jax.experimental.pallas import tpu as pltpu
from jax.sharding import Mesh, PartitionSpec as P

NY, NC, NZ, NX = 4, 2, 16, 4
PLANE = ("y", "c", "x")
NPLANE = NY * NC * NX
MIB = 1 << 20


def vmem():
    return pl.BlockSpec(memory_space=pltpu.VMEM)


def smem():
    return pl.BlockSpec(memory_space=pltpu.SMEM)


def outside():
    return pl.BlockSpec(memory_space=pltpu.HBM)


def anywhere():
    return pl.BlockSpec(memory_space=pl.ANY)


def left_half(rows):
    return lax.broadcasted_iota(jnp.int32, (rows, 128), 1) < 64


def pack_kernel(lists_at, panel_at, scale_at, scaled, payload, extra, lists, panel, scale, blocks, sems):
    fetches = [
        pltpu.make_async_copy(scale_at, scale, sems.at[0]),
        pltpu.make_async_copy(panel_at, panel, sems.at[1]),
        pltpu.make_async_copy(lists_at, lists, sems.at[2]),
    ]
    for fetch in fetches:
        fetch.start()
    for fetch in fetches:
        fetch.wait()
    left = left_half(32)
    for i in range(panel.shape[1] // 128):
        cols = slice(128 * i, 128 * i + 128)
        slab = panel[:, cols].astype(jnp.float32) * scale[i : i + 1, :]
        scaled[:, cols] = slab.astype(jnp.bfloat16)
        top, low = slab[:32], slab[32:]
        turned = pltpu.roll(slab, 64, 1)
        even = jnp.where(left, top, turned[32:])
        odd = jnp.where(left, turned[:32], low)
        blocks[2 * i] = even.astype(jnp.bfloat16)
        blocks[2 * i + 1] = odd.astype(jnp.bfloat16)
    z, x = lax.axis_index("z"), lax.axis_index("x")
    rank = z * NX + x
    for to in range(NX):
        for zz in range(NZ):
            payload[zz * NX + to] = blocks[jnp.maximum(lists[0, zz * NX + to], 0)]
        step = lax.rem(to - x + NX, NX)
        first = lax.rem(rank + step, NZ * NX)
        second = lax.rem(rank + step - NX + NZ * NX, NZ * NX)
        extra[jnp.bitwise_xor(to, x), 0] = blocks[jnp.maximum(lists[1, first], 0)]
        extra[jnp.bitwise_xor(to, x), 1] = blocks[jnp.maximum(lists[1, second], 0)]


def multiply_kernel(where_at, main, near, above, below, scaled, scale, diag, off, halves, gram, table):
    left = left_half(32)

    def spread(at, packed):
        wide = packed.astype(jnp.float32)
        turned = pltpu.roll(wide, 64, 1)
        table[at, :32] = jnp.where(left, wide, turned).astype(jnp.bfloat16)
        table[at, 32:] = jnp.where(left, turned, wide).astype(jnp.bfloat16)

    for s in range(NZ * NX):
        spread(s, main[s])
    for s in range(NX):
        spread(64 + s, near[s, 0])
        spread(68 + s, near[s, 1])
        spread(72 + s, above[s])
        spread(76 + s, below[s])

    left64 = left_half(64)
    for i in range(scaled.shape[1] // 128):
        cols = slice(128 * i, 128 * i + 128)
        rows = []
        own = scaled[:, cols]
        swapped = pltpu.roll(own, 64, 1)
        for b, side in ((2 * i, swapped), (2 * i + 1, own)):
            read = [table[where_at[k, b]] for k in range(5)]
            first = jnp.where(left64, read[0], read[1])
            second = jnp.where(left64, read[2], read[3])
            third = jnp.where(left64, read[4], side)
            rows.append(jnp.concatenate([first, second, third], axis=1))
        weights = [off[k, :, cols] for k in range(5)]
        weights.append(diag[:, cols])
        both = jnp.dot(
            jnp.concatenate(rows, axis=0),
            jnp.concatenate(weights, axis=0),
            preferred_element_type=jnp.float32,
        )
        product = jnp.where(left64, both[:64], both[64:])
        sketch = product * scale[i : i + 1, :]
        high = sketch.astype(jnp.bfloat16)
        low = (sketch - high.astype(jnp.float32)).astype(jnp.bfloat16)
        pair = jnp.concatenate([high, low], axis=0)
        halves[:, cols] = pair
    every = halves[...]
    total = lax.dot_general(every, every, (((1,), (1,)), ((), ())), preferred_element_type=jnp.float32)
    total = total[:64] + total[64:]
    total = total + pltpu.roll(total, 64, 1)
    lane = lax.broadcasted_iota(jnp.int32, (32, 128), 1)
    row = lax.broadcasted_iota(jnp.int32, (32, 128), 0)
    folded = jnp.where((lane & 63) <= row, total[:32], pltpu.roll(total[32:], 32, 1))
    gram[:16] = jnp.where(lane[:16] < 64, folded[:16], folded[16:])
    corner = jnp.where(lane == row + 32, total[32:], 0.0)
    gram[16:] = jnp.sum(corner, axis=0, keepdims=True)


def unfold(packed):
    lane = lax.broadcasted_iota(jnp.int32, (32, 128), 1)
    row = lax.broadcasted_iota(jnp.int32, (32, 128), 0)
    folded = jnp.concatenate([packed[:16], pltpu.roll(packed[:16], 64, 1)], axis=0)
    turned = jnp.concatenate([folded, jnp.zeros((96, 128), jnp.float32)], axis=0).T
    across = jnp.where(lane < 32, turned[:32], pltpu.roll(turned[32:64], 32, 1))
    top = jnp.where(lane <= row, folded, across)
    corner = jnp.where(lane == row + 32, packed[16:], pltpu.roll(turned[:32], 32, 1))
    corner = jnp.where(lane > row + 32, pltpu.roll(folded, 32, 1), corner)
    low = jnp.where(lane < 32, pltpu.roll(folded, 96, 1), corner)
    return jnp.concatenate([top, low], axis=0)


def factor_rows(blocks):
    sub = lax.broadcasted_iota(jnp.int32, (8, 128), 0)
    for p in range(8):
        columns = [
            [jnp.broadcast_to(blocks[r][:, 8 * p + j : 8 * p + j + 1], (8, 128)) for r in range(p, 8)]
            for j in range(8)
        ]
        for j in range(8):
            pivot = jnp.broadcast_to(columns[j][0][j : j + 1], (8, 128))
            inverse = lax.rsqrt(pivot)
            ratio = [c * inverse for c in columns[j]]
            ratio[0] = jnp.where(sub > j, ratio[0], 0.0)
            for t in range(j + 1, 8):
                lead = jnp.broadcast_to(columns[t][0][j : j + 1], (8, 128)) * inverse
                columns[t] = [c - f * lead for c, f in zip(columns[t], ratio)]
            lead = jnp.broadcast_to(blocks[p][j : j + 1], (8, 128)) * inverse
            for r in range(p, 8):
                blocks[r] = blocks[r] - ratio[r - p] * lead
            blocks[p] = jnp.where(sub == j, lead, blocks[p])
    return jnp.concatenate(blocks, axis=0)


def finish_kernel(node_count, gram, halves, basis_at, factor, basis, sems):
    full = unfold(gram[...] * (1.0 / node_count))
    lane = lax.broadcasted_iota(jnp.int32, (64, 128), 1)
    row = lax.broadcasted_iota(jnp.int32, (64, 128), 0)
    work = jnp.where(lane < 64, full, (lane - 64 == row).astype(jnp.float32))
    work = factor_rows([work[8 * r : 8 * r + 8] for r in range(8)])
    factor[...] = jnp.where(row <= lane, work, 0.0)[:, :64]
    solve = pltpu.roll(work, 64, 1)
    solve = jnp.where((lane < 64) & (lane <= row), solve, 0.0)
    high = solve.astype(jnp.bfloat16)
    low = (solve - high.astype(jnp.float32)).astype(jnp.bfloat16)
    twice = jnp.where(lane < 64, solve, pltpu.roll(solve, 64, 1)).astype(jnp.bfloat16)
    left = jnp.concatenate([twice, low], axis=0)
    stores = []
    for i in range(halves.shape[1] // 256):
        cols = slice(256 * i, 256 * i + 256)
        both = jnp.dot(left, halves[:, cols], preferred_element_type=jnp.float32)
        basis[:, cols] = both[:64] + both[64:]
        stores.append(pltpu.make_async_copy(basis.at[:, cols], basis_at.at[:, cols], sems.at[i]))
        stores[-1].start()
    for store in stores:
        store.wait()


def shards(test_panel, node_scale, diag_blocks, off_blocks, block_columns, send_lists):
    panel_width, local_nodes = test_panel.shape
    node_count = local_nodes * NY * NC * NZ * NX
    scale = node_scale.reshape(local_nodes // 128, 128)
    scaled, payload, extra = pl.pallas_call(
        pack_kernel,
        out_shape=(
            jax.ShapeDtypeStruct((64, local_nodes), jnp.bfloat16),
            jax.ShapeDtypeStruct((NZ * NX, 32, 128), jnp.bfloat16),
            jax.ShapeDtypeStruct((NX, 2, 32, 128), jnp.bfloat16),
        ),
        in_specs=[outside(), outside(), outside()],
        out_specs=(vmem(), vmem(), vmem()),
        scratch_shapes=[
            pltpu.SMEM((2, NZ * NX), jnp.int32),
            pltpu.VMEM((64, local_nodes), jnp.bfloat16),
            pltpu.VMEM((local_nodes // 128, 128), jnp.float32),
            pltpu.VMEM((32, 32, 128), jnp.bfloat16),
            pltpu.SemaphoreType.DMA((3,)),
        ],
        name="pack",
    )(send_lists.T, test_panel, scale)

    z, x = lax.axis_index("z"), lax.axis_index("x")
    source, entry = block_columns // 2, block_columns % 2
    source_z, source_x = source // NX, source % NX
    apart = source_x ^ x
    same = 64 + jnp.where(source_x <= x, apart, NX + apart)
    other = jnp.where(source_z == (z + NZ - 1) % NZ, 72, 76) + apart
    where_at = jnp.where(entry == 0, source, jnp.where(source_z == z, same, other))

    main = lax.all_to_all(payload, ("z", "x"), 0, 0, tiled=True)
    moved = [lax.ppermute(extra[d], "x", [(i, i ^ d) for i in range(NX)]) for d in (1, 2, 3)]
    near = jnp.stack([extra[0]] + moved)
    up = [(i, (i + 1) % NZ) for i in range(NZ)]
    down = [((i + 1) % NZ, i) for i in range(NZ)]
    above = lax.ppermute(near[:, 0], "z", up)
    below = lax.ppermute(near[:, 1], "z", down)

    halves, gram = pl.pallas_call(
        multiply_kernel,
        out_shape=(
            jax.ShapeDtypeStruct((128, local_nodes), jnp.bfloat16),
            jax.ShapeDtypeStruct((17, 128), jnp.float32),
        ),
        in_specs=[smem()] + [vmem()] * 8,
        out_specs=(vmem(), vmem()),
        scratch_shapes=[pltpu.VMEM((80, 64, 128), jnp.bfloat16)],
        compiler_params=pltpu.CompilerParams(vmem_limit_bytes=16 * MIB),
        name="multiply",
    )(where_at, main, near, above, below, scaled, scale, diag_blocks, off_blocks)

    def summed(part, axes, count):
        copies = jnp.broadcast_to(part[None, :, None], (count, 17, 1, 128))
        return lax.all_to_all(copies, axes, 0, 0, tiled=True).sum((0, 2))

    gram = summed(summed(gram, PLANE, NPLANE), "z", NZ)

    def finish(*refs):
        finish_kernel(node_count, *refs)

    return pl.pallas_call(
        finish,
        out_shape=(
            jax.ShapeDtypeStruct((64, local_nodes), jnp.float32),
            jax.ShapeDtypeStruct((64, 64), jnp.float32),
        ),
        in_specs=[vmem(), vmem()],
        out_specs=(anywhere(), vmem()),
        scratch_shapes=[
            pltpu.VMEM((64, local_nodes), jnp.float32),
            pltpu.SemaphoreType.DMA((local_nodes // 256,)),
        ],
        compiler_params=pltpu.CompilerParams(vmem_limit_bytes=8 * MIB),
        name="finish",
    )(gram, halves)


def solution(mesh):
    split = Mesh(mesh.devices.reshape(NY, NC, NZ, NX), ("y", "c", "z", "x"))
    every = ("y", "c", "z", "x")
    in_specs = (
        P(None, every),
        P(every),
        P(None, every),
        P(None, None, every),
        P(None, every),
        P(every, None),
    )
    out_specs = (P(None, every), P())
    return jax.shard_map(shards, mesh=split, in_specs=in_specs, out_specs=out_specs, check_vma=False)
```

```python
import jax
import jax.numpy as jnp
from jax import lax
from jax.experimental import pallas as pl
from jax.experimental.pallas import tpu as pltpu
from jax.sharding import Mesh, PartitionSpec as P

NY, NC, NZ, NX = 4, 2, 16, 4
PLANE = ("y", "c", "x")
NPLANE = NY * NC * NX
MIB = 1 << 20


def vmem():
    return pl.BlockSpec(memory_space=pltpu.VMEM)


def smem():
    return pl.BlockSpec(memory_space=pltpu.SMEM)


def outside():
    return pl.BlockSpec(memory_space=pltpu.HBM)


def anywhere():
    return pl.BlockSpec(memory_space=pl.ANY)


def left_half(rows):
    return lax.broadcasted_iota(jnp.int32, (rows, 128), 1) < 64


def pack_kernel(lists_at, panel_at, scale_at, scaled, payload, extra, lists, panel, scale, blocks, sems):
    fetches = [
        pltpu.make_async_copy(scale_at, scale, sems.at[0]),
        pltpu.make_async_copy(panel_at, panel, sems.at[1]),
        pltpu.make_async_copy(lists_at, lists, sems.at[2]),
    ]
    for fetch in fetches:
        fetch.start()
    for fetch in fetches:
        fetch.wait()
    left = left_half(32)
    for i in range(panel.shape[1] // 128):
        cols = slice(128 * i, 128 * i + 128)
        slab = panel[:, cols].astype(jnp.float32) * scale[i : i + 1, :]
        scaled[:, cols] = slab.astype(jnp.bfloat16)
        top, low = slab[:32], slab[32:]
        turned = pltpu.roll(slab, 64, 1)
        even = jnp.where(left, top, turned[32:])
        odd = jnp.where(left, turned[:32], low)
        blocks[2 * i] = even.astype(jnp.bfloat16)
        blocks[2 * i + 1] = odd.astype(jnp.bfloat16)
    z, x = lax.axis_index("z"), lax.axis_index("x")
    rank = z * NX + x
    for to in range(NX):
        for zz in range(NZ):
            payload[zz * NX + to] = blocks[jnp.maximum(lists[0, zz * NX + to], 0)]
        step = lax.rem(to - x + NX, NX)
        first = lax.rem(rank + step, NZ * NX)
        second = lax.rem(rank + step - NX + NZ * NX, NZ * NX)
        extra[jnp.bitwise_xor(to, x), 0] = blocks[jnp.maximum(lists[1, first], 0)]
        extra[jnp.bitwise_xor(to, x), 1] = blocks[jnp.maximum(lists[1, second], 0)]


def multiply_kernel(where_at, main, near, above, below, scaled, scale, diag, off, halves, gram, table):
    left = left_half(32)

    def spread(at, packed):
        wide = packed.astype(jnp.float32)
        turned = pltpu.roll(wide, 64, 1)
        table[at, :32] = jnp.where(left, wide, turned).astype(jnp.bfloat16)
        table[at, 32:] = jnp.where(left, turned, wide).astype(jnp.bfloat16)

    for s in range(NZ * NX):
        spread(s, main[s])
    for s in range(NX):
        spread(64 + s, near[s, 0])
        spread(68 + s, near[s, 1])
        spread(72 + s, above[s])
        spread(76 + s, below[s])

    left64 = left_half(64)
    for i in range(scaled.shape[1] // 128):
        cols = slice(128 * i, 128 * i + 128)
        rows = []
        own = scaled[:, cols]
        swapped = pltpu.roll(own, 64, 1)
        for b, side in ((2 * i, swapped), (2 * i + 1, own)):
            read = [table[where_at[k, b]] for k in range(5)]
            first = jnp.where(left64, read[0], read[1])
            second = jnp.where(left64, read[2], read[3])
            third = jnp.where(left64, read[4], side)
            rows.append(jnp.concatenate([first, second, third], axis=1))
        weights = [off[k, :, cols] for k in range(5)]
        weights.append(diag[:, cols])
        both = jnp.dot(
            jnp.concatenate(rows, axis=0),
            jnp.concatenate(weights, axis=0),
            preferred_element_type=jnp.float32,
        )
        product = jnp.where(left64, both[:64], both[64:])
        sketch = product * scale[i : i + 1, :]
        high = sketch.astype(jnp.bfloat16)
        low = (sketch - high.astype(jnp.float32)).astype(jnp.bfloat16)
        pair = jnp.concatenate([high, low], axis=0)
        halves[:, cols] = pair
    every = halves[...]
    total = lax.dot_general(every, every, (((1,), (1,)), ((), ())), preferred_element_type=jnp.float32)
    total = total[:64] + total[64:]
    total = total + pltpu.roll(total, 64, 1)
    lane = lax.broadcasted_iota(jnp.int32, (32, 128), 1)
    row = lax.broadcasted_iota(jnp.int32, (32, 128), 0)
    folded = jnp.where((lane & 63) <= row, total[:32], pltpu.roll(total[32:], 32, 1))
    gram[:16] = jnp.where(lane[:16] < 64, folded[:16], folded[16:])
    corner = jnp.where(lane == row + 32, total[32:], 0.0)
    gram[16:] = jnp.sum(corner, axis=0, keepdims=True)


def unfold(packed):
    lane = lax.broadcasted_iota(jnp.int32, (32, 128), 1)
    row = lax.broadcasted_iota(jnp.int32, (32, 128), 0)
    folded = jnp.concatenate([packed[:16], pltpu.roll(packed[:16], 64, 1)], axis=0)
    turned = jnp.concatenate([folded, jnp.zeros((96, 128), jnp.float32)], axis=0).T
    across = jnp.where(lane < 32, turned[:32], pltpu.roll(turned[32:64], 32, 1))
    top = jnp.where(lane <= row, folded, across)
    corner = jnp.where(lane == row + 32, packed[16:], pltpu.roll(turned[:32], 32, 1))
    corner = jnp.where(lane > row + 32, pltpu.roll(folded, 32, 1), corner)
    low = jnp.where(lane < 32, pltpu.roll(folded, 96, 1), corner)
    return jnp.concatenate([top, low], axis=0)


def factor_rows(blocks, nothing):
    sub = lax.broadcasted_iota(jnp.int32, (8, 128), 0)
    for p in range(8):
        columns = [
            [blocks[r][:, 8 * p + j : 8 * p + j + 1] + nothing for r in range(p, 8)]
            for j in range(8)
        ]
        for j in range(8):
            pivot = jnp.broadcast_to(columns[j][0][j : j + 1], (8, 128))
            inverse = lax.rsqrt(pivot)
            ratio = [c * inverse for c in columns[j]]
            ratio[0] = jnp.where(sub > j, ratio[0], 0.0)
            for t in range(j + 1, 8):
                lead = jnp.broadcast_to(columns[t][0][j : j + 1], (8, 128)) * inverse
                columns[t] = [c - f * lead for c, f in zip(columns[t], ratio)]
            lead = jnp.broadcast_to(blocks[p][j : j + 1], (8, 128)) * inverse
            for r in range(p, 8):
                blocks[r] = blocks[r] - ratio[r - p] * lead
            blocks[p] = jnp.where(sub == j, lead, blocks[p])
    return jnp.concatenate(blocks, axis=0)


def finish_kernel(node_count, gram, halves, basis_at, factor_at, basis, factor, sems):
    full = unfold(gram[...] * (1.0 / node_count))
    lane = lax.broadcasted_iota(jnp.int32, (64, 128), 1)
    row = lax.broadcasted_iota(jnp.int32, (64, 128), 0)
    work = jnp.where(lane < 64, full, (lane - 64 == row).astype(jnp.float32))
    work = factor_rows([work[8 * r : 8 * r + 8] for r in range(8)], full[:8] * 0.0)
    factor[...] = jnp.where(row <= lane, work, 0.0)[:, :64]
    stores = [pltpu.make_async_copy(factor, factor_at, sems.at[halves.shape[1] // 256])]
    stores[0].start()
    solve = pltpu.roll(work, 64, 1)
    solve = jnp.where((lane < 64) & (lane <= row), solve, 0.0)
    high = solve.astype(jnp.bfloat16)
    low = (solve - high.astype(jnp.float32)).astype(jnp.bfloat16)
    twice = jnp.where(lane < 64, solve, pltpu.roll(solve, 64, 1)).astype(jnp.bfloat16)
    left = jnp.concatenate([twice, low], axis=0)
    for i in range(halves.shape[1] // 256):
        cols = slice(256 * i, 256 * i + 256)
        both = jnp.dot(left, halves[:, cols], preferred_element_type=jnp.float32)
        basis[:, cols] = both[:64] + both[64:]
        stores.append(pltpu.make_async_copy(basis.at[:, cols], basis_at.at[:, cols], sems.at[i]))
        stores[-1].start()
    for store in stores:
        store.wait()


def shards(test_panel, node_scale, diag_blocks, off_blocks, block_columns, send_lists):
    panel_width, local_nodes = test_panel.shape
    node_count = local_nodes * NY * NC * NZ * NX
    scale = node_scale.reshape(local_nodes // 128, 128)
    scaled, payload, extra = pl.pallas_call(
        pack_kernel,
        out_shape=(
            jax.ShapeDtypeStruct((64, local_nodes), jnp.bfloat16),
            jax.ShapeDtypeStruct((NZ * NX, 32, 128), jnp.bfloat16),
            jax.ShapeDtypeStruct((NX, 2, 32, 128), jnp.bfloat16),
        ),
        in_specs=[outside(), outside(), outside()],
        out_specs=(vmem(), vmem(), vmem()),
        scratch_shapes=[
            pltpu.SMEM((2, NZ * NX), jnp.int32),
            pltpu.VMEM((64, local_nodes), jnp.bfloat16),
            pltpu.VMEM((local_nodes // 128, 128), jnp.float32),
            pltpu.VMEM((32, 32, 128), jnp.bfloat16),
            pltpu.SemaphoreType.DMA((3,)),
        ],
        name="pack",
    )(send_lists.T, test_panel, scale)

    z, x = lax.axis_index("z"), lax.axis_index("x")
    source, entry = block_columns // 2, block_columns % 2
    source_z, source_x = source // NX, source % NX
    apart = source_x ^ x
    same = 64 + jnp.where(source_x <= x, apart, NX + apart)
    other = jnp.where(source_z == (z + NZ - 1) % NZ, 72, 76) + apart
    where_at = jnp.where(entry == 0, source, jnp.where(source_z == z, same, other))

    main = lax.all_to_all(payload, ("z", "x"), 0, 0, tiled=True)
    moved = [lax.ppermute(extra[d], "x", [(i, i ^ d) for i in range(NX)]) for d in (1, 2, 3)]
    near = jnp.stack([extra[0]] + moved)
    up = [(i, (i + 1) % NZ) for i in range(NZ)]
    down = [((i + 1) % NZ, i) for i in range(NZ)]
    above = lax.ppermute(near[:, 0], "z", up)
    below = lax.ppermute(near[:, 1], "z", down)

    halves, gram = pl.pallas_call(
        multiply_kernel,
        out_shape=(
            jax.ShapeDtypeStruct((128, local_nodes), jnp.bfloat16),
            jax.ShapeDtypeStruct((17, 128), jnp.float32),
        ),
        in_specs=[smem()] + [vmem()] * 8,
        out_specs=(vmem(), vmem()),
        scratch_shapes=[pltpu.VMEM((80, 64, 128), jnp.bfloat16)],
        compiler_params=pltpu.CompilerParams(vmem_limit_bytes=16 * MIB),
        name="multiply",
    )(where_at, main, near, above, below, scaled, scale, diag_blocks, off_blocks)

    def summed(part, axes, count):
        copies = jnp.broadcast_to(part[None, :, None], (count, 17, 1, 128))
        return lax.all_to_all(copies, axes, 0, 0, tiled=True).sum((0, 2))

    gram = summed(summed(gram, PLANE, NPLANE), "z", NZ)

    def finish(*refs):
        finish_kernel(node_count, *refs)

    return pl.pallas_call(
        finish,
        out_shape=(
            jax.ShapeDtypeStruct((64, local_nodes), jnp.float32),
            jax.ShapeDtypeStruct((64, 64), jnp.float32),
        ),
        in_specs=[vmem(), vmem()],
        out_specs=(anywhere(), anywhere()),
        scratch_shapes=[
            pltpu.VMEM((64, local_nodes), jnp.float32),
            pltpu.VMEM((64, 64), jnp.float32),
            pltpu.SemaphoreType.DMA((local_nodes // 256 + 1,)),
        ],
        compiler_params=pltpu.CompilerParams(vmem_limit_bytes=8 * MIB),
        name="finish",
    )(gram, halves)


def solution(mesh):
    split = Mesh(mesh.devices.reshape(NY, NC, NZ, NX), ("y", "c", "z", "x"))
    every = ("y", "c", "z", "x")
    in_specs = (
        P(None, every),
        P(every),
        P(None, every),
        P(None, None, every),
        P(None, every),
        P(every, None),
    )
    out_specs = (P(None, every), P())
    return jax.shard_map(shards, mesh=split, in_specs=in_specs, out_specs=out_specs, check_vma=False)
```

```python
import jax
import jax.numpy as jnp
from jax import lax
from jax.experimental import pallas as pl
from jax.experimental.pallas import tpu as pltpu
from jax.sharding import Mesh, PartitionSpec as P

NY, NC, NZ, NX = 4, 2, 16, 4
PLANE = ("y", "c", "x")
NPLANE = NY * NC * NX
MIB = 1 << 20


def vmem():
    return pl.BlockSpec(memory_space=pltpu.VMEM)


def smem():
    return pl.BlockSpec(memory_space=pltpu.SMEM)


def outside():
    return pl.BlockSpec(memory_space=pltpu.HBM)


def anywhere():
    return pl.BlockSpec(memory_space=pl.ANY)


def left_half(rows):
    return lax.broadcasted_iota(jnp.int32, (rows, 128), 1) < 64


def pack_kernel(lists_at, panel_at, scale_at, payload, extra, lists, panel, scale, blocks, sems):
    fetches = [
        pltpu.make_async_copy(scale_at, scale, sems.at[0]),
        pltpu.make_async_copy(panel_at, panel, sems.at[1]),
        pltpu.make_async_copy(lists_at, lists, sems.at[2]),
    ]
    for fetch in fetches:
        fetch.start()
    for fetch in fetches:
        fetch.wait()
    left = left_half(32)
    for i in range(panel.shape[1] // 128):
        cols = slice(128 * i, 128 * i + 128)
        slab = panel[:, cols].astype(jnp.float32) * scale[i : i + 1, :]
        top, low = slab[:32], slab[32:]
        turned = pltpu.roll(slab, 64, 1)
        even = jnp.where(left, top, turned[32:])
        odd = jnp.where(left, turned[:32], low)
        blocks[2 * i] = even.astype(jnp.bfloat16)
        blocks[2 * i + 1] = odd.astype(jnp.bfloat16)
    z, x = lax.axis_index("z"), lax.axis_index("x")
    rank = z * NX + x
    for to in range(NX):
        for zz in range(NZ):
            payload[zz * NX + to] = blocks[jnp.maximum(lists[0, zz * NX + to], 0)]
        step = lax.rem(to - x + NX, NX)
        first = lax.rem(rank + step, NZ * NX)
        second = lax.rem(rank + step - NX + NZ * NX, NZ * NX)
        extra[jnp.bitwise_xor(to, x), 0] = blocks[jnp.maximum(lists[1, first], 0)]
        extra[jnp.bitwise_xor(to, x), 1] = blocks[jnp.maximum(lists[1, second], 0)]


def multiply_kernel(where_at, main, near, above, below, panel, scale, diag, off, halves, gram, table):
    left = left_half(32)

    def spread(at, packed):
        wide = packed.astype(jnp.float32)
        turned = pltpu.roll(wide, 64, 1)
        table[at, :32] = jnp.where(left, wide, turned).astype(jnp.bfloat16)
        table[at, 32:] = jnp.where(left, turned, wide).astype(jnp.bfloat16)

    for s in range(NZ * NX):
        spread(s, main[s])
    for s in range(NX):
        spread(64 + s, near[s, 0])
        spread(68 + s, near[s, 1])
        spread(72 + s, above[s])
        spread(76 + s, below[s])

    left64 = left_half(64)
    for i in range(panel.shape[1] // 128):
        cols = slice(128 * i, 128 * i + 128)
        rows = []
        own = (panel[:, cols].astype(jnp.float32) * scale[i : i + 1, :]).astype(jnp.bfloat16)
        swapped = pltpu.roll(own, 64, 1)
        for b, side in ((2 * i, swapped), (2 * i + 1, own)):
            read = [table[where_at[k, b]] for k in range(5)]
            first = jnp.where(left64, read[0], read[1])
            second = jnp.where(left64, read[2], read[3])
            third = jnp.where(left64, read[4], side)
            rows.append(jnp.concatenate([first, second, third], axis=1))
        weights = [off[k, :, cols] for k in range(5)]
        weights.append(diag[:, cols])
        both = jnp.dot(
            jnp.concatenate(rows, axis=0),
            jnp.concatenate(weights, axis=0),
            preferred_element_type=jnp.float32,
        )
        product = jnp.where(left64, both[:64], both[64:])
        sketch = product * scale[i : i + 1, :]
        high = sketch.astype(jnp.bfloat16)
        low = (sketch - high.astype(jnp.float32)).astype(jnp.bfloat16)
        pair = jnp.concatenate([high, low], axis=0)
        halves[:, cols] = pair
    every = halves[...]
    total = lax.dot_general(every, every, (((1,), (1,)), ((), ())), preferred_element_type=jnp.float32)
    total = total[:64] + total[64:]
    total = total + pltpu.roll(total, 64, 1)
    lane = lax.broadcasted_iota(jnp.int32, (32, 128), 1)
    row = lax.broadcasted_iota(jnp.int32, (32, 128), 0)
    folded = jnp.where((lane & 63) <= row, total[:32], pltpu.roll(total[32:], 32, 1))
    gram[:16] = jnp.where(lane[:16] < 64, folded[:16], folded[16:])
    corner = jnp.where(lane == row + 32, total[32:], 0.0)
    gram[16:] = jnp.sum(corner, axis=0, keepdims=True)


def unfold(packed):
    lane = lax.broadcasted_iota(jnp.int32, (32, 128), 1)
    row = lax.broadcasted_iota(jnp.int32, (32, 128), 0)
    folded = jnp.concatenate([packed[:16], pltpu.roll(packed[:16], 64, 1)], axis=0)
    turned = jnp.concatenate([folded, jnp.zeros((96, 128), jnp.float32)], axis=0).T
    across = jnp.where(lane < 32, turned[:32], pltpu.roll(turned[32:64], 32, 1))
    top = jnp.where(lane <= row, folded, across)
    corner = jnp.where(lane == row + 32, packed[16:], pltpu.roll(turned[:32], 32, 1))
    corner = jnp.where(lane > row + 32, pltpu.roll(folded, 32, 1), corner)
    low = jnp.where(lane < 32, pltpu.roll(folded, 96, 1), corner)
    return jnp.concatenate([top, low], axis=0)


def factor_rows(blocks, nothing):
    sub = lax.broadcasted_iota(jnp.int32, (8, 128), 0)
    for p in range(8):
        columns = [
            [blocks[r][:, 8 * p + j : 8 * p + j + 1] + nothing for r in range(p, 8)]
            for j in range(8)
        ]
        for j in range(8):
            pivot = jnp.broadcast_to(columns[j][0][j : j + 1], (8, 128))
            inverse = lax.rsqrt(pivot)
            ratio = [c * inverse for c in columns[j]]
            ratio[0] = jnp.where(sub > j, ratio[0], 0.0)
            for t in range(j + 1, 8):
                lead = jnp.broadcast_to(columns[t][0][j : j + 1], (8, 128)) * inverse
                columns[t] = [c - f * lead for c, f in zip(columns[t], ratio)]
            lead = jnp.broadcast_to(blocks[p][j : j + 1], (8, 128)) * inverse
            for r in range(p, 8):
                blocks[r] = blocks[r] - ratio[r - p] * lead
            blocks[p] = jnp.where(sub == j, lead, blocks[p])
    return jnp.concatenate(blocks, axis=0)


def finish_kernel(node_count, gram, halves, basis_at, factor_at, basis, factor, sems):
    full = unfold(gram[...] * (1.0 / node_count))
    lane = lax.broadcasted_iota(jnp.int32, (64, 128), 1)
    row = lax.broadcasted_iota(jnp.int32, (64, 128), 0)
    work = jnp.where(lane < 64, full, (lane - 64 == row).astype(jnp.float32))
    work = factor_rows([work[8 * r : 8 * r + 8] for r in range(8)], full[:8] * 0.0)
    factor[...] = jnp.where(row <= lane, work, 0.0)[:, :64]
    stores = [pltpu.make_async_copy(factor, factor_at, sems.at[halves.shape[1] // 256])]
    stores[0].start()
    solve = pltpu.roll(work, 64, 1)
    solve = jnp.where((lane < 64) & (lane <= row), solve, 0.0)
    high = solve.astype(jnp.bfloat16)
    low = (solve - high.astype(jnp.float32)).astype(jnp.bfloat16)
    twice = jnp.where(lane < 64, solve, pltpu.roll(solve, 64, 1)).astype(jnp.bfloat16)
    left = jnp.concatenate([twice, low], axis=0)
    for i in range(halves.shape[1] // 256):
        cols = slice(256 * i, 256 * i + 256)
        both = jnp.dot(left, halves[:, cols], preferred_element_type=jnp.float32)
        basis[:, cols] = both[:64] + both[64:]
        stores.append(pltpu.make_async_copy(basis.at[:, cols], basis_at.at[:, cols], sems.at[i]))
        stores[-1].start()
    for store in stores:
        store.wait()


def shards(test_panel, node_scale, diag_blocks, off_blocks, block_columns, send_lists):
    panel_width, local_nodes = test_panel.shape
    node_count = local_nodes * NY * NC * NZ * NX
    scale = node_scale.reshape(local_nodes // 128, 128)
    payload, extra = pl.pallas_call(
        pack_kernel,
        out_shape=(
            jax.ShapeDtypeStruct((NZ * NX, 32, 128), jnp.bfloat16),
            jax.ShapeDtypeStruct((NX, 2, 32, 128), jnp.bfloat16),
        ),
        in_specs=[outside(), outside(), outside()],
        out_specs=(vmem(), vmem()),
        scratch_shapes=[
            pltpu.SMEM((2, NZ * NX), jnp.int32),
            pltpu.VMEM((64, local_nodes), jnp.bfloat16),
            pltpu.VMEM((local_nodes // 128, 128), jnp.float32),
            pltpu.VMEM((32, 32, 128), jnp.bfloat16),
            pltpu.SemaphoreType.DMA((3,)),
        ],
        name="pack",
    )(send_lists.T, test_panel, scale)

    z, x = lax.axis_index("z"), lax.axis_index("x")
    source, entry = block_columns // 2, block_columns % 2
    source_z, source_x = source // NX, source % NX
    apart = source_x ^ x
    same = 64 + jnp.where(source_x <= x, apart, NX + apart)
    other = jnp.where(source_z == (z + NZ - 1) % NZ, 72, 76) + apart
    where_at = jnp.where(entry == 0, source, jnp.where(source_z == z, same, other))

    main = lax.all_to_all(payload, ("z", "x"), 0, 0, tiled=True)
    moved = [lax.ppermute(extra[d], "x", [(i, i ^ d) for i in range(NX)]) for d in (1, 2, 3)]
    near = jnp.stack([extra[0]] + moved)
    up = [(i, (i + 1) % NZ) for i in range(NZ)]
    down = [((i + 1) % NZ, i) for i in range(NZ)]
    above = lax.ppermute(near[:, 0], "z", up)
    below = lax.ppermute(near[:, 1], "z", down)

    halves, gram = pl.pallas_call(
        multiply_kernel,
        out_shape=(
            jax.ShapeDtypeStruct((128, local_nodes), jnp.bfloat16),
            jax.ShapeDtypeStruct((17, 128), jnp.float32),
        ),
        in_specs=[smem()] + [vmem()] * 8,
        out_specs=(vmem(), vmem()),
        scratch_shapes=[pltpu.VMEM((80, 64, 128), jnp.bfloat16)],
        compiler_params=pltpu.CompilerParams(vmem_limit_bytes=16 * MIB),
        name="multiply",
    )(where_at, main, near, above, below, test_panel, scale, diag_blocks, off_blocks)

    def summed(part, axes, count):
        copies = jnp.broadcast_to(part[None, :, None], (count, 17, 1, 128))
        return lax.all_to_all(copies, axes, 0, 0, tiled=True).sum((0, 2))

    gram = summed(summed(gram, PLANE, NPLANE), "z", NZ)

    def finish(*refs):
        finish_kernel(node_count, *refs)

    return pl.pallas_call(
        finish,
        out_shape=(
            jax.ShapeDtypeStruct((64, local_nodes), jnp.float32),
            jax.ShapeDtypeStruct((64, 64), jnp.float32),
        ),
        in_specs=[vmem(), vmem()],
        out_specs=(anywhere(), anywhere()),
        scratch_shapes=[
            pltpu.VMEM((64, local_nodes), jnp.float32),
            pltpu.VMEM((64, 64), jnp.float32),
            pltpu.SemaphoreType.DMA((local_nodes // 256 + 1,)),
        ],
        compiler_params=pltpu.CompilerParams(vmem_limit_bytes=8 * MIB),
        name="finish",
    )(gram, halves)


def solution(mesh):
    split = Mesh(mesh.devices.reshape(NY, NC, NZ, NX), ("y", "c", "z", "x"))
    every = ("y", "c", "z", "x")
    in_specs = (
        P(None, every),
        P(every),
        P(None, every),
        P(None, None, every),
        P(None, every),
        P(every, None),
    )
    out_specs = (P(None, every), P())
    return jax.shard_map(shards, mesh=split, in_specs=in_specs, out_specs=out_specs, check_vma=False)
```

```python
import jax
import jax.numpy as jnp
from jax import lax
from jax.experimental import pallas as pl
from jax.experimental.pallas import tpu as pltpu
from jax.sharding import Mesh, PartitionSpec as P

NY, NC, NZ, NX = 4, 2, 16, 4
NZL = 8
Z = ("zh", "zl")
PLANE = ("y", "c", "x")
NPLANE = NY * NC * NX
MIB = 1 << 20


def vmem():
    return pl.BlockSpec(memory_space=pltpu.VMEM)


def smem():
    return pl.BlockSpec(memory_space=pltpu.SMEM)


def outside():
    return pl.BlockSpec(memory_space=pltpu.HBM)


def anywhere():
    return pl.BlockSpec(memory_space=pl.ANY)


def place(z, x):
    return (z // NZL * NX + x) * NZL + z % NZL


def left_half(rows):
    return lax.broadcasted_iota(jnp.int32, (rows, 128), 1) < 64


def pack_kernel(lists_at, panel_at, scale_at, payload, extra, lists, panel, scale, blocks, sems):
    fetches = [
        pltpu.make_async_copy(scale_at, scale, sems.at[0]),
        pltpu.make_async_copy(panel_at, panel, sems.at[1]),
        pltpu.make_async_copy(lists_at, lists, sems.at[2]),
    ]
    for fetch in fetches:
        fetch.start()
    for fetch in fetches:
        fetch.wait()
    left = left_half(32)
    for i in range(panel.shape[1] // 128):
        cols = slice(128 * i, 128 * i + 128)
        slab = panel[:, cols].astype(jnp.float32) * scale[i : i + 1, :]
        slab = slab.astype(jnp.bfloat16)
        turned = pltpu.roll(slab, 64, 1)
        blocks[2 * i] = jnp.where(left, slab[:32], turned[32:])
        blocks[2 * i + 1] = jnp.where(left, turned[:32], slab[32:])
    z, x = lax.axis_index("zh") * NZL + lax.axis_index("zl"), lax.axis_index("x")
    rank = z * NX + x
    for to in range(NX):
        for zz in range(NZ):
            payload[place(zz, to)] = blocks[jnp.maximum(lists[0, zz * NX + to], 0)]
        step = lax.rem(to - x + NX, NX)
        first = lax.rem(rank + step, NZ * NX)
        second = lax.rem(rank + step - NX + NZ * NX, NZ * NX)
        extra[jnp.bitwise_xor(to, x), 0] = blocks[jnp.maximum(lists[1, first], 0)]
        extra[jnp.bitwise_xor(to, x), 1] = blocks[jnp.maximum(lists[1, second], 0)]


def multiply_kernel(where_at, main, near, above, below, panel, scale, diag, off, halves, gram, table):
    left = left_half(32)

    def spread(at, packed):
        wide = packed.astype(jnp.float32)
        turned = pltpu.roll(wide, 64, 1)
        table[at, :32] = jnp.where(left, wide, turned).astype(jnp.bfloat16)
        table[at, 32:] = jnp.where(left, turned, wide).astype(jnp.bfloat16)

    for s in range(NZ * NX):
        spread(s, main[place(s // NX, s % NX)])
    for s in range(NX):
        spread(64 + s, near[s, 0])
        spread(68 + s, near[s, 1])
        spread(72 + s, above[s])
        spread(76 + s, below[s])

    left64 = left_half(64)
    for i in range(panel.shape[1] // 128):
        cols = slice(128 * i, 128 * i + 128)
        rows = []
        own = (panel[:, cols].astype(jnp.float32) * scale[i : i + 1, :]).astype(jnp.bfloat16)
        swapped = pltpu.roll(own, 64, 1)
        for b, side in ((2 * i, swapped), (2 * i + 1, own)):
            read = [table[where_at[k, b]] for k in range(5)]
            first = jnp.where(left64, read[0], read[1])
            second = jnp.where(left64, read[2], read[3])
            third = jnp.where(left64, read[4], side)
            rows.append(jnp.concatenate([first, second, third], axis=1))
        weights = [off[k, :, cols] for k in range(5)]
        weights.append(diag[:, cols])
        both = jnp.dot(
            jnp.concatenate(rows, axis=0),
            jnp.concatenate(weights, axis=0),
            preferred_element_type=jnp.float32,
        )
        product = jnp.where(left64, both[:64], both[64:])
        sketch = product * scale[i : i + 1, :]
        high = sketch.astype(jnp.bfloat16)
        low = (sketch - high.astype(jnp.float32)).astype(jnp.bfloat16)
        pair = jnp.concatenate([high, low], axis=0)
        halves[:, cols] = pair
    every = halves[...]
    total = lax.dot_general(every, every, (((1,), (1,)), ((), ())), preferred_element_type=jnp.float32)
    total = total[:64] + total[64:]
    total = total + pltpu.roll(total, 64, 1)
    lane = lax.broadcasted_iota(jnp.int32, (32, 128), 1)
    row = lax.broadcasted_iota(jnp.int32, (32, 128), 0)
    folded = jnp.where((lane & 63) <= row, total[:32], pltpu.roll(total[32:], 32, 1))
    gram[:16] = jnp.where(lane[:16] < 64, folded[:16], folded[16:])
    corner = jnp.where(lane == row + 32, total[32:], 0.0)
    gram[16:] = jnp.sum(corner, axis=0, keepdims=True)


def unfold(packed):
    lane = lax.broadcasted_iota(jnp.int32, (32, 128), 1)
    row = lax.broadcasted_iota(jnp.int32, (32, 128), 0)
    folded = jnp.concatenate([packed[:16], pltpu.roll(packed[:16], 64, 1)], axis=0)
    turned = jnp.concatenate([folded, jnp.zeros((96, 128), jnp.float32)], axis=0).T
    across = jnp.where(lane < 32, turned[:32], pltpu.roll(turned[32:64], 32, 1))
    top = jnp.where(lane <= row, folded, across)
    corner = jnp.where(lane == row + 32, packed[16:], pltpu.roll(turned[:32], 32, 1))
    corner = jnp.where(lane > row + 32, pltpu.roll(folded, 32, 1), corner)
    low = jnp.where(lane < 32, pltpu.roll(folded, 96, 1), corner)
    return jnp.concatenate([top, low], axis=0)


def factor_rows(blocks, nothing):
    sub = lax.broadcasted_iota(jnp.int32, (8, 128), 0)
    for p in range(8):
        columns = [
            [blocks[r][:, 8 * p + j : 8 * p + j + 1] + nothing for r in range(p, 8)]
            for j in range(8)
        ]
        for j in range(8):
            pivot = jnp.broadcast_to(columns[j][0][j : j + 1], (8, 128))
            inverse = lax.rsqrt(pivot)
            ratio = [c * inverse for c in columns[j]]
            ratio[0] = jnp.where(sub > j, ratio[0], 0.0)
            for t in range(j + 1, 8):
                lead = jnp.broadcast_to(columns[t][0][j : j + 1], (8, 128)) * inverse
                columns[t] = [c - f * lead for c, f in zip(columns[t], ratio)]
            lead = jnp.broadcast_to(blocks[p][j : j + 1], (8, 128)) * inverse
            for r in range(p, 8):
                blocks[r] = blocks[r] - ratio[r - p] * lead
            blocks[p] = jnp.where(sub == j, lead, blocks[p])
    return jnp.concatenate(blocks, axis=0)


def finish_kernel(node_count, gram, halves, basis_at, factor_at, basis, factor, sems):
    full = unfold(gram[...] * (1.0 / node_count))
    lane = lax.broadcasted_iota(jnp.int32, (64, 128), 1)
    row = lax.broadcasted_iota(jnp.int32, (64, 128), 0)
    work = jnp.where(lane < 64, full, (lane - 64 == row).astype(jnp.float32))
    work = factor_rows([work[8 * r : 8 * r + 8] for r in range(8)], full[:8] * 0.0)
    factor[...] = jnp.where(row <= lane, work, 0.0)[:, :64]
    stores = [pltpu.make_async_copy(factor, factor_at, sems.at[halves.shape[1] // 256])]
    stores[0].start()
    solve = pltpu.roll(work, 64, 1)
    solve = jnp.where((lane < 64) & (lane <= row), solve, 0.0)
    high = solve.astype(jnp.bfloat16)
    low = (solve - high.astype(jnp.float32)).astype(jnp.bfloat16)
    twice = jnp.where(lane < 64, solve, pltpu.roll(solve, 64, 1)).astype(jnp.bfloat16)
    left = jnp.concatenate([twice, low], axis=0)
    for i in range(halves.shape[1] // 256):
        cols = slice(256 * i, 256 * i + 256)
        both = jnp.dot(left, halves[:, cols], preferred_element_type=jnp.float32)
        basis[:, cols] = both[:64] + both[64:]
        stores.append(pltpu.make_async_copy(basis.at[:, cols], basis_at.at[:, cols], sems.at[i]))
        stores[-1].start()
    for store in stores:
        store.wait()


def shards(test_panel, node_scale, diag_blocks, off_blocks, block_columns, send_lists):
    panel_width, local_nodes = test_panel.shape
    node_count = local_nodes * NY * NC * NZ * NX
    scale = node_scale.reshape(local_nodes // 128, 128)
    payload, extra = pl.pallas_call(
        pack_kernel,
        out_shape=(
            jax.ShapeDtypeStruct((NZ * NX, 32, 128), jnp.bfloat16),
            jax.ShapeDtypeStruct((NX, 2, 32, 128), jnp.bfloat16),
        ),
        in_specs=[outside(), outside(), outside()],
        out_specs=(vmem(), vmem()),
        scratch_shapes=[
            pltpu.SMEM((2, NZ * NX), jnp.int32),
            pltpu.VMEM((64, local_nodes), jnp.bfloat16),
            pltpu.VMEM((local_nodes // 128, 128), jnp.float32),
            pltpu.VMEM((32, 32, 128), jnp.bfloat16),
            pltpu.SemaphoreType.DMA((3,)),
        ],
        name="pack",
    )(send_lists.T, test_panel, scale)

    z, x = lax.axis_index("zh") * NZL + lax.axis_index("zl"), lax.axis_index("x")
    source, entry = block_columns // 2, block_columns % 2
    source_z, source_x = source // NX, source % NX
    apart = source_x ^ x
    same = 64 + jnp.where(source_x <= x, apart, NX + apart)
    other = jnp.where(source_z == (z + NZ - 1) % NZ, 72, 76) + apart
    where_at = jnp.where(entry == 0, source, jnp.where(source_z == z, same, other))

    main = lax.all_to_all(payload, ("zh", "x", "zl"), 0, 0, tiled=True)
    moved = [lax.ppermute(extra[d], "x", [(i, i ^ d) for i in range(NX)]) for d in (1, 2, 3)]
    near = jnp.stack([extra[0]] + moved)
    up = [(i, (i + 1) % NZ) for i in range(NZ)]
    down = [((i + 1) % NZ, i) for i in range(NZ)]
    above = lax.ppermute(near[:, 0], Z, up)
    below = lax.ppermute(near[:, 1], Z, down)

    halves, gram = pl.pallas_call(
        multiply_kernel,
        out_shape=(
            jax.ShapeDtypeStruct((128, local_nodes), jnp.bfloat16),
            jax.ShapeDtypeStruct((17, 128), jnp.float32),
        ),
        in_specs=[smem()] + [vmem()] * 8,
        out_specs=(vmem(), vmem()),
        scratch_shapes=[pltpu.VMEM((80, 64, 128), jnp.bfloat16)],
        compiler_params=pltpu.CompilerParams(vmem_limit_bytes=16 * MIB),
        name="multiply",
    )(where_at, main, near, above, below, test_panel, scale, diag_blocks, off_blocks)

    def summed(part, axes, count):
        copies = jnp.broadcast_to(part[None, :, None], (count, 17, 1, 128))
        return lax.all_to_all(copies, axes, 0, 0, tiled=True).sum((0, 2))

    gram = summed(summed(gram, PLANE, NPLANE), Z, NZ)

    def finish(*refs):
        finish_kernel(node_count, *refs)

    return pl.pallas_call(
        finish,
        out_shape=(
            jax.ShapeDtypeStruct((64, local_nodes), jnp.float32),
            jax.ShapeDtypeStruct((64, 64), jnp.float32),
        ),
        in_specs=[vmem(), vmem()],
        out_specs=(anywhere(), anywhere()),
        scratch_shapes=[
            pltpu.VMEM((64, local_nodes), jnp.float32),
            pltpu.VMEM((64, 64), jnp.float32),
            pltpu.SemaphoreType.DMA((local_nodes // 256 + 1,)),
        ],
        compiler_params=pltpu.CompilerParams(vmem_limit_bytes=8 * MIB),
        name="finish",
    )(gram, halves)


def solution(mesh):
    split = Mesh(mesh.devices.reshape(NY, NC, NZ // NZL, NZL, NX), ("y", "c", "zh", "zl", "x"))
    every = ("y", "c", "zh", "zl", "x")
    in_specs = (
        P(None, every),
        P(every),
        P(None, every),
        P(None, None, every),
        P(None, every),
        P(every, None),
    )
    out_specs = (P(None, every), P())
    return jax.shard_map(shards, mesh=split, in_specs=in_specs, out_specs=out_specs, check_vma=False)
```
